32 devices in a mesh: seq: 16 (over z, x, core), batch: 2 (over y).
Axes of the slice: x: 2, y: 2, z: 4, core: 2. Of those that a mesh axis runs over, the one named last changes fastest.
Arguments:
- queries: bfloat16 [8192, 2048], P(('batch', 'seq')), parts along dimension 0, may hold values from -9 to 9
- key_rows: bfloat16 [8192, 2048], P(('batch', 'seq')), parts along dimension 0, may hold values from -9 to 9
- values: bfloat16 [8192, 2048], P(('batch', 'seq')), parts along dimension 0, may hold values from -6 to 6
- bias_tiles: bfloat16 [3, 256, 256], replicated, may hold values from -6 to 6
- buckets: int32 [5], replicated, may hold values from 0 to 2
- slopes: float32 [32], replicated, may hold values from 0.3 to 1.5
Outputs:
- attended: bfloat16 [8192, 2048], P(('batch', 'seq')), parts along dimension 0
The draws below stay inside these ranges and needn't reach their ends.
There are 2 independent parts, one for each index of `batch`. The reference program is written for one: setup_inputs(seed, part) draws one part's arguments, and reference() takes and returns one part's arrays. A program takes and returns all parts, laid end to end along the dimension named above; an argument that names none is the same for every part. Nothing has to cross between parts.
All inputs are finite; a program needn't handle non-finite values.
Results may differ from the reference program's by a relative error of at most 0.0043.
Values may be sent and summed in bfloat16 or wider, within the bound.
No kernel may reach another device: no remote copies, remote signals or barrier semaphores. Data moves between devices by JAX's collectives and lax.ppermute only.
A program may use at most 128 MiB of HBM per device.

```python
import math
import jax
import jax.numpy as jnp
from jax import lax

H = 32
HD = 64
TOK_DEV = 256
WIN = 4
NBUCKET = 3
D = 2048
LEN = 4096


def base_draw(key, salt):
    return jnp.clip(jax.random.normal(jax.random.fold_in(key, salt), (LEN, H * HD), jnp.float32), -6.0, 6.0)


def draw_queries(key, part):
    result = base_draw(key, 1)
    return result.astype(jnp.bfloat16)


def draw_key_rows(key, part):
    result = base_draw(key, 2)
    return result.astype(jnp.bfloat16)


def with_ends(values, own_key, low, largest):
    spot = [jax.random.randint(jax.random.fold_in(own_key, axis), (), 0, length) for axis, length in enumerate(values.shape)]
    longest = values.shape.index(max(values.shape))
    beside = spot[:longest] + [(spot[longest] + 1) % values.shape[longest]] + spot[longest + 1:]
    return values.at[tuple(spot)].set(low).at[tuple(beside)].set(largest)


def shard_levels(own_key, dims, split, smallest, high):
    def one(position, shards_of):
        draws = jax.random.uniform(jax.random.fold_in(jax.random.fold_in(own_key, 6), position), (shards_of,), jnp.float32, smallest / len(split), high / len(split))
        return jnp.repeat(jnp.exp(draws), dims[position] // shards_of).reshape((-1,) + (1,) * (len(dims) - position - 1))

    level = one(*split[0])
    for cut in split[1:]:
        level = level * one(*cut)
    return level


def normal_values(key, extent, width, most, split=(), held_as=jnp.bfloat16):
    array = jax.random.normal(key, extent, jnp.float32) * width
    if len(split) > 0:
        array = shard_levels(key, extent, split, -0.22, 0.18) * array
    return jnp.clip(array, min=-most, max=most).astype(held_as)


def setup_inputs(seed: int = 0, part: int = 0) -> dict:
    key_list = jax.random.split(jax.random.key(seed), 7)
    part_splits = jax.random.split(jax.random.fold_in(key_list[6], part), 7)
    queries = draw_queries(jax.random.fold_in(jax.random.fold_in(key_list[6], part), 71), part)
    key_rows = draw_key_rows(jax.random.fold_in(jax.random.fold_in(key_list[6], part), 71), part)
    values = normal_values(part_splits[2], (LEN, D), 1.0, 6.0, ((0, 16),))
    bias_tiles = normal_values(key_list[3], (NBUCKET, TOK_DEV, TOK_DEV), 1.0, 6.0)
    buckets = with_ends(jax.random.randint(key_list[4], (WIN + 1,), 0, NBUCKET), jax.random.fold_in(key_list[4], 1), 0, NBUCKET - 1).astype(jnp.int32)
    slopes = jnp.clip(jnp.exp(jax.random.uniform(key_list[5], (H,), jnp.float32, math.log(0.3), math.log(1.5))), 0.3, 1.5)
    return dict(queries=queries, key_rows=key_rows, values=values, bias_tiles=bias_tiles, buckets=buckets, slopes=slopes)


def window_bias(bias_tiles, buckets):
    pieces = []
    for offset in range(-WIN, WIN + 1):
        tile = bias_tiles[buckets[abs(offset)]].astype(jnp.float32)
        if offset < 0:
            tile = tile.T
        pieces.append(tile)
    return jnp.concatenate(pieces, axis=1)


def block_attention(query_part, key_part, value_part, bias_window, slope_part):
    head_count = slope_part.shape[0]
    head_width = query_part.shape[1] // head_count
    group_size = min(head_count, 4)
    group_count = head_count // group_size
    row_count = query_part.shape[0]
    key_count = key_part.shape[0]
    query_groups = query_part.reshape(row_count, group_count, group_size, head_width).transpose(1, 0, 2, 3)
    key_groups = key_part.reshape(key_count, group_count, group_size, head_width).transpose(1, 0, 2, 3)
    value_groups = value_part.reshape(key_count, group_count, group_size, head_width).transpose(1, 0, 2, 3)
    slope_groups = slope_part.reshape(group_count, group_size)

    def per_group(packed):
        query_one, key_one, value_one, slope_one = packed
        scores = jnp.einsum("qgd,kgd->gqk", query_one.astype(jnp.float32), key_one.astype(jnp.float32))
        scores = scores * (HD ** -0.5) + slope_one.astype(jnp.float32)[:, None, None] * bias_window[None]
        peaks = jnp.max(scores, axis=-1, keepdims=True)
        raised = jnp.exp(scores - peaks)
        totals = jnp.sum(raised, axis=-1)
        weights = lax.optimization_barrier(raised.astype(jnp.bfloat16))
        weighted = jnp.einsum("gqk,kgd->qgd", weights.astype(jnp.float32), value_one.astype(jnp.float32))
        return (weighted / totals.T[:, :, None]).astype(jnp.bfloat16)

    results = lax.map(per_group, (query_groups, key_groups, value_groups, slope_groups))
    return results.transpose(1, 0, 2, 3).reshape(row_count, head_count * head_width)


def reference(queries, key_rows, values, bias_tiles, buckets, slopes):
    bias_window = window_bias(bias_tiles, buckets)
    block_total = queries.shape[0] // TOK_DEV
    width_all = queries.shape[1]
    key_blocks = key_rows.reshape(block_total, TOK_DEV, width_all)
    value_blocks = values.reshape(block_total, TOK_DEV, width_all)
    offsets = jnp.arange(-WIN, WIN + 1, dtype=jnp.int32)

    def per_block(block):
        query_part = lax.dynamic_slice_in_dim(queries, (block * TOK_DEV).astype(jnp.int32), TOK_DEV, 0)
        chosen = ((block + offsets) % block_total).astype(jnp.int32)
        key_part = key_blocks[chosen].reshape(-1, width_all)
        value_part = value_blocks[chosen].reshape(-1, width_all)
        return block_attention(query_part, key_part, value_part, bias_window, slopes)

    results = lax.map(per_block, jnp.arange(block_total, dtype=jnp.int32))
    return results.reshape(block_total * TOK_DEV, width_all)
```

```python
import functools

import jax
import jax.numpy as jnp
from jax import lax
from jax.experimental import pallas as pl
from jax.experimental.pallas import tpu as pltpu
from jax.sharding import PartitionSpec as P

LANES = 128


def bias_kernel(win, buckets, tile_ref, out_ref):
    step = pl.program_id(0)
    tile = tile_ref[0].astype(jnp.float32)

    @pl.when(step < win)
    def _():
        out_ref[0] = tile.T

    @pl.when(step >= win)
    def _():
        out_ref[0] = tile


def bias_window(bias_tiles, buckets):
    win = buckets.shape[0] - 1
    block_len = bias_tiles.shape[1]
    grid_spec = pltpu.PrefetchScalarGridSpec(
        num_scalar_prefetch=1,
        grid=(2 * win + 1,),
        in_specs=[
            pl.BlockSpec(
                (1, block_len, block_len), lambda t, b: (b[jnp.abs(t - win)], 0, 0)
            )
        ],
        out_specs=pl.BlockSpec((1, block_len, block_len), lambda t, b: (t, 0, 0)),
    )
    return pl.pallas_call(
        functools.partial(bias_kernel, win),
        grid_spec=grid_spec,
        out_shape=jax.ShapeDtypeStruct((2 * win + 1, block_len, block_len), jnp.float32),
        name="bias_window",
    )(buckets, bias_tiles)


def pack_kernel(groups, *refs):
    count = sum(len(g) for g in groups)
    ins, outs = refs[:count], refs[count:]
    at = 0
    for group, out in zip(groups, outs):
        for slot in range(len(group)):
            out[0, slot] = ins[at][...]
            at += 1


def pack(arrays, groups, plane, name):
    rows = arrays[0].shape[0]
    flat = [item for group in groups for item in group]
    in_specs = [
        pl.BlockSpec((rows, LANES), functools.partial(lambda c, p: (0, plane * c + p), chunk))
        for _, chunk in flat
    ]
    out_specs = [
        pl.BlockSpec((1, len(g), rows, LANES), lambda p: (p, 0, 0, 0)) for g in groups
    ]
    out_shape = [
        jax.ShapeDtypeStruct((plane, len(g), rows, LANES), arrays[0].dtype) for g in groups
    ]
    size = sum(len(g) for g in groups) * plane * rows * LANES * 4
    return pl.pallas_call(
        functools.partial(pack_kernel, groups),
        grid=(plane,),
        in_specs=in_specs,
        out_specs=out_specs,
        out_shape=out_shape,
        cost_estimate=pl.CostEstimate(flops=0, bytes_accessed=size, transcendentals=0),
        name=name,
    )(*[arrays[a] for a, _ in flat])


def attention_kernel(
    win, heads, scale, slopes, q_ref, up_ref, own_ref, down_ref, bias_ref, out_ref,
    kv, scores, sems,
):
    step = pl.program_id(0)
    plane = own_ref.shape[0]
    rows = q_ref.shape[2]
    head_width = LANES // heads

    @pl.when(step == 0)
    def _():
        copies = [
            pltpu.make_async_copy(ref, kv.at[pl.ds(plane * at, plane)], sems.at[at])
            for at, ref in enumerate((up_ref, own_ref, down_ref))
        ]
        for copy in copies:
            copy.start()
        for copy in copies:
            copy.wait()

    base = step + plane - win
    query = q_ref[0, 0] * jnp.asarray(scale, q_ref.dtype)
    lane = lax.broadcasted_iota(jnp.int32, (1, LANES), 1) // head_width
    tiles = 2 * win + 1
    result = jnp.zeros((rows, LANES), jnp.float32)
    for head in range(heads):
        slope = slopes[head]
        mine = lane == head
        one = jnp.where(mine, query, jnp.zeros_like(query))
        best = None
        for t in range(tiles):
            keys = kv[base + t, 0]
            tile = lax.dot_general(
                one, keys, (((1,), (1,)), ((), ())), preferred_element_type=jnp.float32
            )
            tile = tile + slope * bias_ref[t]
            scores[:, t * rows:(t + 1) * rows] = tile
            for at in range(0, rows, LANES):
                part = tile[:, at:at + LANES]
                best = part if best is None else jnp.maximum(best, part)
        peak = jnp.max(best, axis=1, keepdims=True)
        total = jnp.zeros((rows, LANES), jnp.float32)
        acc = jnp.zeros((rows, LANES), jnp.float32)
        for t in range(tiles):
            raised = jnp.exp(scores[:, t * rows:(t + 1) * rows] - peak)
            for at in range(0, rows, LANES):
                total = total + raised[:, at:at + LANES]
            acc = acc + jnp.dot(
                raised.astype(q_ref.dtype), kv[base + t, 1], preferred_element_type=jnp.float32
            )
        acc = acc / jnp.sum(total, axis=1, keepdims=True)
        result = jnp.where(mine, acc, result)
    out_ref[0] = result.astype(out_ref.dtype)


def attention(query, chunk, up, own, down, bias, slopes, head_width):
    plane, _, rows, _ = query.shape
    tiles = bias.shape[0]
    win = tiles // 2
    heads = LANES // head_width
    any_spec = pl.BlockSpec(memory_space=pl.ANY)
    pairs = plane * tiles * heads * rows * rows
    grid_spec = pltpu.PrefetchScalarGridSpec(
        num_scalar_prefetch=1,
        grid=(plane,),
        in_specs=[
            pl.BlockSpec((1, 1, rows, LANES), lambda i, s: (i, chunk, 0, 0)),
            any_spec, any_spec, any_spec,
            pl.BlockSpec(bias.shape, lambda i, s: (0, 0, 0), pipeline_mode=pl.Buffered(1)),
        ],
        out_specs=pl.BlockSpec((1, rows, LANES), lambda i, s: (i, 0, 0)),
        scratch_shapes=[
            pltpu.VMEM((3 * plane, 2, rows, LANES), query.dtype),
            pltpu.VMEM((rows, tiles * rows), jnp.float32),
            pltpu.SemaphoreType.DMA((3,)),
        ],
    )
    return pl.pallas_call(
        functools.partial(attention_kernel, win, heads, head_width ** -0.5),
        grid_spec=grid_spec,
        out_shape=jax.ShapeDtypeStruct((plane, rows, LANES), query.dtype),
        cost_estimate=pl.CostEstimate(
            flops=4 * pairs * LANES, bytes_accessed=8 << 20, transcendentals=pairs
        ),
        compiler_params=pltpu.CompilerParams(vmem_limit_bytes=32 << 20),
        name="attention",
    )(slopes, query, up, own, down, bias)


def unpack_kernel(count, *refs):
    out = refs[count]
    for at in range(count):
        out[:, at * LANES:(at + 1) * LANES] = refs[at][0]


def unpack(parts):
    plane, rows, _ = parts[0].shape
    return jnp.concatenate([p.transpose(1, 0, 2).reshape(rows, plane * LANES) for p in parts], axis=1)


def per_device(queries, key_rows, values, bias_tiles, buckets, slopes):
    count = lax.axis_size("seq")
    plane = buckets.shape[0] - 1
    width = queries.shape[1]
    head_width = width // slopes.shape[0]
    chunks = width // (plane * LANES)
    heads = LANES // head_width
    planes = [[g * plane + p for p in range(plane)] for g in range(count // plane)]
    onward = [(i, (i + plane) % count) for i in range(count)]
    back = [(i, (i - plane) % count) for i in range(count)]

    def swap(x):
        return lax.all_to_all(
            x, "seq", split_axis=0, concat_axis=0, tiled=True, axis_index_groups=planes
        )

    def up(x):
        return lax.ppermute(x, "seq", onward)

    def down(x):
        return lax.ppermute(x, "seq", back)

    place = lax.axis_index("seq") % plane
    local_slopes = lax.dynamic_slice_in_dim(
        slopes.reshape(chunks, plane, heads), place, 1, 1
    )[:, 0]

    (first,) = pack((key_rows, values), [[(0, 0), (1, 0)]], plane, "pack_first")
    raw_up, raw_down = up(first), down(first)
    rest = pack(
        (queries, key_rows, values),
        [[(1, c), (2, c)] for c in range(1, chunks)] + [[(0, c) for c in range(chunks)]],
        plane,
        "pack_rest",
    )
    own = [None] + [swap(x) for x in rest[:-1]]
    query = swap(rest[-1])
    own[0] = swap(first)
    bias = bias_window(bias_tiles, buckets)
    ups = [swap(raw_up)] + [up(x) for x in own[1:]]
    downs = [swap(raw_down)] + [down(x) for x in own[1:]]
    parts = [
        swap(attention(query, c, ups[c], own[c], downs[c], bias, local_slopes[c], head_width))
        for c in range(chunks)
    ]
    return unpack(parts)


def solution(mesh):
    rows = P(("batch", "seq"), None)
    return jax.shard_map(
        per_device,
        mesh=mesh,
        in_specs=(rows, rows, rows, P(), P(), P()),
        out_specs=rows,
        check_vma=False,
    )
```

```python
import functools

import jax
import jax.numpy as jnp
from jax import lax
from jax.experimental import pallas as pl
from jax.experimental.pallas import tpu as pltpu
from jax.sharding import PartitionSpec as P


LANES = 128
FULL = 67043328
ANY = pl.BlockSpec(memory_space=pl.ANY)
SMEM = pl.BlockSpec(memory_space=pltpu.SMEM)
PARAMS = pltpu.CompilerParams(vmem_limit_bytes=FULL)


def bias_kernel(win, buckets, tile_ref, near_ref, far_ref):
    for t in range(-win, win + 1):
        tile = tile_ref[buckets[abs(t)]].astype(jnp.float32)
        if t < win:
            near_ref[t + win] = tile.T if t < 0 else tile
        if t > 0:
            far_ref[t - 1] = tile


def bias_window(bias_tiles, buckets):
    win = buckets.shape[0] - 1
    side = bias_tiles.shape[1]
    vmem = pl.BlockSpec(memory_space=pltpu.VMEM)
    return pl.pallas_call(
        functools.partial(bias_kernel, win),
        in_specs=[SMEM, vmem],
        out_specs=[vmem, vmem],
        out_shape=[
            jax.ShapeDtypeStruct((2 * win, side, side), jnp.float32),
            jax.ShapeDtypeStruct((win, side, side), jnp.float32),
        ],
        compiler_params=PARAMS,
        name="bias_window",
    )(buckets, bias_tiles)


def columns(place, chunk, plane):
    return pl.ds(pl.multiple_of((place + chunk * plane) * LANES, LANES), LANES)


def pack_kernel(plane, groups, names, place_ref, *refs):
    ins, outs = refs[:len(names)], refs[len(names):-3]
    held, sem_in, sem_out = refs[-3:]
    place = place_ref[0]
    width = plane * LANES
    slots = sorted({item for group in groups for item in group})
    loads, stores = {}, []
    for at, (array, chunk) in enumerate(slots):
        loads[array, chunk] = copy = pltpu.make_async_copy(
            ins[names.index(array)].at[:, pl.ds(chunk * width, width)], held.at[at], sem_in.at[at]
        )
        copy.start()
    waited = set()
    for g, group in enumerate(groups):
        for slot, item in enumerate(group):
            if item not in waited:
                loads[item].wait()
                waited.add(item)
            for k in range(plane):
                copy = pltpu.make_async_copy(
                    held.at[slots.index(item), :, columns(place ^ k, 0, plane)],
                    outs[g * plane + k].at[slot],
                    sem_out.at[len(stores)],
                )
                copy.start()
                stores.append(copy)
    for copy in stores:
        copy.wait()


def pack(arrays, groups, plane, place):
    names = list(arrays)
    first = arrays[names[0]]
    rows = first.shape[0]
    slots = len({item for g in groups for item in g})
    stores = plane * sum(len(g) for g in groups)
    outs = pl.pallas_call(
        functools.partial(pack_kernel, plane, groups, names),
        in_specs=[SMEM] + [ANY] * len(names),
        out_specs=[ANY] * (plane * len(groups)),
        out_shape=[
            jax.ShapeDtypeStruct((len(g), rows, LANES), first.dtype)
            for g in groups for _ in range(plane)
        ],
        scratch_shapes=[
            pltpu.VMEM((slots, rows, plane * LANES), first.dtype),
            pltpu.SemaphoreType.DMA((slots,)),
            pltpu.SemaphoreType.DMA((stores,)),
        ],
        cost_estimate=pl.CostEstimate(
            flops=0, bytes_accessed=stores * rows * LANES * 4, transcendentals=0
        ),
        compiler_params=PARAMS,
    )(place, *arrays.values())
    return [outs[g * plane:(g + 1) * plane] for g in range(len(groups))]


def unpack_kernel(plane, chunk0, chunks, count, place_ref, *refs):
    ins, (out, held, sem_in, sem_out) = refs[:count * plane], refs[-4:]
    place = place_ref[0]
    width = plane * LANES
    at, loads = 0, []
    for group in range(count):
        for chunk in range(ins[group * plane].shape[0]):
            for k in range(plane):
                copy = pltpu.make_async_copy(
                    ins[group * plane + k].at[chunk],
                    held.at[at, :, columns(place ^ k, 0, plane)],
                    sem_in.at[at, k],
                )
                copy.start()
                loads.append(copy)
            at += 1
    stores = []
    for at in range(chunks):
        for copy in loads[at * plane:(at + 1) * plane]:
            copy.wait()
        copy = pltpu.make_async_copy(
            held.at[at], out.at[:, pl.ds((chunk0 + at) * width, width)], sem_out.at[at]
        )
        copy.start()
        stores.append(copy)
    for copy in stores:
        copy.wait()


def unpack(place, groups, chunk0, total, into):
    plane = len(groups[0])
    chunks = sum(g[0].shape[0] for g in groups)
    _, rows, _ = groups[0][0].shape
    dtype = groups[0][0].dtype
    flat = [x for g in groups for x in g]
    extra = [] if into is None else [into]
    return pl.pallas_call(
        functools.partial(unpack_kernel, plane, chunk0, chunks, len(groups)),
        in_specs=[SMEM] + [ANY] * (len(flat) + len(extra)),
        out_specs=ANY,
        out_shape=jax.ShapeDtypeStruct((rows, total * plane * LANES), dtype),
        scratch_shapes=[
            pltpu.VMEM((chunks, rows, plane * LANES), dtype),
            pltpu.SemaphoreType.DMA((chunks, plane)),
            pltpu.SemaphoreType.DMA((chunks,)),
        ],
        input_output_aliases={} if into is None else {1 + len(flat): 0},
        cost_estimate=pl.CostEstimate(
            flops=0, bytes_accessed=chunks * rows * plane * LANES * 4, transcendentals=0
        ),
        compiler_params=PARAMS,
    )(place, *flat, *extra)


def scores(query, tiles, slope, store):
    best = None
    for at, (keys, _, bias) in enumerate(tiles):
        tile = lax.dot_general(
            query, keys[...], (((1,), (1,)), ((), ())), preferred_element_type=jnp.float32
        )
        tile = tile + slope * bias[...]
        store[at] = tile
        for lane in range(0, tile.shape[1], LANES):
            part = tile[:, lane:lane + LANES]
            best = part if best is None else jnp.maximum(best, part)
    return jnp.broadcast_to(jnp.max(best, axis=1, keepdims=True), best.shape)


def weigh(tiles, peak, store, dtype):
    acc = None
    for at, (_, values, _) in enumerate(tiles):
        raised = jnp.concatenate(
            [
                jnp.exp(store[at, :, lane:lane + LANES] - peak).astype(dtype)
                for lane in range(0, store.shape[2], LANES)
            ],
            axis=1,
        )
        part = jnp.dot(raised, values[...], preferred_element_type=jnp.float32)
        acc = part if acc is None else acc + part
    return acc


def lanes_of(head_width, head):
    return lax.broadcasted_iota(jnp.int32, (1, LANES), 1) // head_width == head


def near_kernel(win, plane, chunk0, head_width, place_ref, slopes, *refs):
    qs = refs[:plane]
    uks, uvs = refs[plane:2 * plane], refs[2 * plane:3 * plane]
    oks, ovs = refs[3 * plane:4 * plane], refs[4 * plane:5 * plane]
    bias, acc_ref, peak_ref, store, keys, ones, query = refs[5 * plane:]
    place = place_ref[0]
    heads = LANES // head_width
    chunk, head = pl.program_id(0) + chunk0, pl.program_id(1)
    dtype = keys.dtype
    slope = slopes[(chunk * plane + place) * heads + head]
    mine = lanes_of(head_width, head)
    scale = jnp.asarray(head_width ** -0.5, dtype)
    for k in range(plane):
        at = place ^ k
        query[at] = jnp.where(mine, qs[k][0] * scale, jnp.zeros((), dtype))
        ones[at] = jnp.where(mine, uvs[k][0], jnp.ones((), dtype))
        ones[plane + at] = jnp.where(mine, ovs[k][0], jnp.ones((), dtype))
        keys[at] = uks[k][0]
        keys[plane + at] = oks[k][0]
    for i in range(plane):
        tiles = []
        for b in range(2 * plane):
            offset = b - plane - i
            if offset >= -win:
                tiles.append((keys.at[b], ones.at[b], bias.at[offset + win]))
        slot = store.at[i % 2]
        peak = scores(query[i], tiles, slope, slot)
        peak_ref[0, 0, i] = peak
        acc_ref[0, 0, i] = weigh(tiles, peak, slot, dtype)


def near(place, slopes, qs, ups, owns, bias, chunk0, chunks, total, head_width):
    plane = len(qs)
    _, rows, _ = qs[0].shape
    win = bias.shape[0] // 2
    heads = LANES // head_width
    block = (1, rows, LANES)
    pairs = chunks * heads * rows * rows * (plane * plane + plane * (plane + 1) // 2)
    key_spec = pl.BlockSpec(block, lambda c, h: (c, 0, 0))
    value_spec = pl.BlockSpec(block, lambda c, h: (chunks + c, 0, 0))
    query_spec = pl.BlockSpec(block, lambda c, h: (chunk0 + c, 0, 0))
    own_key = pl.BlockSpec(block, lambda c, h: (chunk0 + c, 0, 0))
    own_value = pl.BlockSpec(block, lambda c, h: (total + chunk0 + c, 0, 0))
    out = (chunks, heads, plane, rows, LANES)
    out_spec = pl.BlockSpec((1, 1) + out[2:], lambda c, h: (c, h, 0, 0, 0))
    return pl.pallas_call(
        functools.partial(near_kernel, win, plane, chunk0, head_width),
        grid=(chunks, heads),
        in_specs=[SMEM, SMEM] + [query_spec] * plane + [key_spec] * plane + [value_spec] * plane
        + [own_key] * plane + [own_value] * plane
        + [pl.BlockSpec(bias.shape, lambda c, h: (0, 0, 0), pipeline_mode=pl.Buffered(1))],
        out_specs=[out_spec, out_spec],
        out_shape=[jax.ShapeDtypeStruct(out, jnp.float32)] * 2,
        scratch_shapes=[
            pltpu.VMEM((2, 2 * win, rows, rows), jnp.float32),
            pltpu.VMEM((2 * plane, rows, LANES), qs[0].dtype),
            pltpu.VMEM((2 * plane, rows, LANES), qs[0].dtype),
            pltpu.VMEM((plane, rows, LANES), qs[0].dtype),
        ],
        cost_estimate=pl.CostEstimate(
            flops=4 * pairs * LANES, bytes_accessed=chunks * (4 << 20), transcendentals=pairs
        ),
        compiler_params=PARAMS,
        name="near",
    )(place, slopes, *qs, *ups, *ups, *owns, *owns, bias)


def far_kernel(win, plane, chunk0, head_width, place_ref, slopes, *refs):
    qs, dks, dvs = (refs[n * plane:(n + 1) * plane] for n in range(3))
    bias, acc_ref, peak_ref = refs[3 * plane:3 * plane + 3]
    outs = refs[3 * plane + 3:4 * plane + 3]
    store, keys, ones, query, held = refs[4 * plane + 3:]
    place = place_ref[0]
    heads = LANES // head_width
    chunk = pl.program_id(0) + chunk0
    dtype = keys.dtype
    scale = jnp.asarray(head_width ** -0.5, dtype)
    for k in range(plane):
        at = place ^ k
        keys[at] = dks[k][0]
        for head in range(heads):
            mine = lanes_of(head_width, head)
            query[head, at] = jnp.where(mine, qs[k][0] * scale, jnp.zeros((), dtype))
            ones[head, at] = jnp.where(mine, dvs[k][0], jnp.ones((), dtype))
    for i in range(plane):
        upper = lower = None
        for head in range(heads):
            slope = slopes[(chunk * plane + place) * heads + head]
            tiles = [
                (keys.at[b], ones.at[head, b], bias.at[b + plane - i - 1])
                for b in range(plane) if b + plane - i <= win
            ]
            slot = store.at[(i * heads + head) % store.shape[0]]
            before = peak_ref[0, head, i]
            peak = jnp.maximum(scores(query[head, i], tiles, slope, slot), before)
            acc = weigh(tiles, peak, slot, dtype) + acc_ref[0, head, i] * jnp.exp(before - peak)
            if upper is None:
                upper, lower = acc, acc
            else:
                mine = lanes_of(head_width, head)
                beside = lanes_of(head_width, head - 1)
                upper = jnp.where(mine, acc, upper)
                lower = jnp.where(beside, acc, lower)
        lower = pltpu.roll(lower, head_width, 1)
        held[i ^ place] = (upper / lower).astype(dtype)
    for k in range(plane):
        outs[k][0] = held[k]


def far(place, slopes, qs, downs, bias, before, chunk0, chunks, head_width):
    plane = len(qs)
    _, rows, _ = qs[0].shape
    win = bias.shape[0]
    heads = LANES // head_width
    block = (1, rows, LANES)
    pairs = chunks * heads * rows * rows * (plane * (plane + 1) // 2)
    acc, peak, base = before
    key_spec = pl.BlockSpec(block, lambda c: (c, 0, 0))
    value_spec = pl.BlockSpec(block, lambda c: (chunks + c, 0, 0))
    query_spec = pl.BlockSpec(block, lambda c: (chunk0 + c, 0, 0))
    near_spec = pl.BlockSpec(
        (1, heads, plane, rows, LANES), lambda c: (chunk0 - base + c, 0, 0, 0, 0)
    )
    return pl.pallas_call(
        functools.partial(far_kernel, win, plane, chunk0, head_width),
        grid=(chunks,),
        in_specs=[SMEM, SMEM] + [query_spec] * plane + [key_spec] * plane + [value_spec] * plane
        + [pl.BlockSpec(bias.shape, lambda c: (0, 0, 0), pipeline_mode=pl.Buffered(1))]
        + [near_spec, near_spec],
        out_specs=[key_spec] * plane,
        out_shape=[jax.ShapeDtypeStruct((chunks, rows, LANES), qs[0].dtype)] * plane,
        scratch_shapes=[
            pltpu.VMEM((2 * heads, win, rows, rows), jnp.float32),
            pltpu.VMEM((plane, rows, LANES), qs[0].dtype),
            pltpu.VMEM((heads, plane, rows, LANES), qs[0].dtype),
            pltpu.VMEM((heads, plane, rows, LANES), qs[0].dtype),
            pltpu.VMEM((plane, rows, LANES), qs[0].dtype),
        ],
        cost_estimate=pl.CostEstimate(
            flops=4 * pairs * LANES, bytes_accessed=chunks * (4 << 20), transcendentals=pairs
        ),
        compiler_params=PARAMS,
        name="far",
    )(place, slopes, *qs, *downs, *downs, bias, acc, peak)


def per_device(queries, key_rows, values, bias_tiles, buckets, slopes):
    count = lax.axis_size("seq")
    plane = buckets.shape[0] - 1
    width = queries.shape[1]
    head_width = width // slopes.shape[0]
    chunks = width // (plane * LANES)

    def send(arrays, step):
        out = []
        for k, x in enumerate(arrays):
            if k == 0 and step == 0:
                out.append(x)
                continue
            pairs = [(i, ((i + step * plane) % count) ^ k) for i in range(count)]
            out.append(lax.ppermute(x, "seq", pairs))
        return out

    place = (lax.axis_index("seq") % plane).astype(jnp.int32).reshape(1)
    data = dict(q=queries, k=key_rows, v=values)

    def kv(start, size):
        span = range(start, start + size)
        return [("k", c) for c in span] + [("v", c) for c in span]

    groups = [(0, chunks - 2), (chunks - 2, 1), (chunks - 1, 1)]
    kv_only = dict(k=key_rows, v=values)
    (packed,) = pack(kv_only, [kv(0, chunks)], plane, place)
    rest = pack(data, [[("q", c) for c in range(chunks)]] + [kv(*g) for g in groups], plane, place)
    ups = send(packed, 1)
    qs = send(rest[0], 0)
    owns = send(packed, 0)
    near_bias, far_bias = bias_window(bias_tiles, buckets)
    downs = [send(x, -1) for x in rest[1:]]
    sums = near(place, slopes, qs, ups, owns, near_bias, 0, chunks, chunks, head_width)
    back = []
    for g, (start, size) in enumerate(groups):
        outs = far(place, slopes, qs, downs[g], far_bias, (*sums, 0), start, size, head_width)
        back.append(send(outs, 0))
    most = unpack(place, back[:1], 0, chunks, None)
    return unpack(place, back[1:], chunks - 2, chunks, most)


def solution(mesh):
    rows = P(("batch", "seq"), None)
    return jax.shard_map(
        per_device,
        mesh=mesh,
        in_specs=(rows, rows, rows, P(), P(), P()),
        out_specs=rows,
        check_vma=False,
    )
```

```python
import functools

import jax
import jax.numpy as jnp
from jax import lax
from jax.experimental import pallas as pl
from jax.experimental.pallas import tpu as pltpu
from jax.sharding import PartitionSpec as P


LANES = 128
FULL = 67043328
ANY = pl.BlockSpec(memory_space=pl.ANY)
SMEM = pl.BlockSpec(memory_space=pltpu.SMEM)
PARAMS = pltpu.CompilerParams(vmem_limit_bytes=FULL)


def bias_kernel(win, buckets, tile_ref, near_ref, far_ref):
    for t in range(-win, win + 1):
        tile = tile_ref[buckets[abs(t)]].astype(jnp.float32)
        if t < win:
            near_ref[t + win] = tile.T if t < 0 else tile
        if t > 0:
            far_ref[t - 1] = tile


def bias_window(bias_tiles, buckets):
    win = buckets.shape[0] - 1
    side = bias_tiles.shape[1]
    vmem = pl.BlockSpec(memory_space=pltpu.VMEM)
    return pl.pallas_call(
        functools.partial(bias_kernel, win),
        in_specs=[SMEM, vmem],
        out_specs=[vmem, vmem],
        out_shape=[
            jax.ShapeDtypeStruct((2 * win, side, side), jnp.float32),
            jax.ShapeDtypeStruct((win, side, side), jnp.float32),
        ],
        compiler_params=PARAMS,
        name="bias_window",
    )(buckets, bias_tiles)


def columns(place, chunk, plane):
    return pl.ds(pl.multiple_of((place + chunk * plane) * LANES, LANES), LANES)


def pack_kernel(plane, groups, names, place_ref, *refs):
    ins, outs = refs[:len(names)], refs[len(names):-3]
    held, sem_in, sem_out = refs[-3:]
    place = place_ref[0]
    width = plane * LANES
    slots = sorted({item for group in groups for item in group})
    loads, stores = {}, []
    for at, (array, chunk) in enumerate(slots):
        loads[array, chunk] = copy = pltpu.make_async_copy(
            ins[names.index(array)].at[:, pl.ds(chunk * width, width)], held.at[at], sem_in.at[at]
        )
        copy.start()
    waited = set()
    for g, group in enumerate(groups):
        for slot, item in enumerate(group):
            if item not in waited:
                loads[item].wait()
                waited.add(item)
            for k in range(plane):
                copy = pltpu.make_async_copy(
                    held.at[slots.index(item), :, columns(place ^ k, 0, plane)],
                    outs[g * plane + k].at[slot],
                    sem_out.at[len(stores)],
                )
                copy.start()
                stores.append(copy)
    for copy in stores:
        copy.wait()


def pack(arrays, groups, plane, place):
    names = list(arrays)
    first = arrays[names[0]]
    rows = first.shape[0]
    slots = len({item for g in groups for item in g})
    stores = plane * sum(len(g) for g in groups)
    outs = pl.pallas_call(
        functools.partial(pack_kernel, plane, groups, names),
        in_specs=[SMEM] + [ANY] * len(names),
        out_specs=[ANY] * (plane * len(groups)),
        out_shape=[
            jax.ShapeDtypeStruct((len(g), rows, LANES), first.dtype)
            for g in groups for _ in range(plane)
        ],
        scratch_shapes=[
            pltpu.VMEM((slots, rows, plane * LANES), first.dtype),
            pltpu.SemaphoreType.DMA((slots,)),
            pltpu.SemaphoreType.DMA((stores,)),
        ],
        cost_estimate=pl.CostEstimate(
            flops=0, bytes_accessed=stores * rows * LANES * 4, transcendentals=0
        ),
        compiler_params=PARAMS,
    )(place, *arrays.values())
    return [outs[g * plane:(g + 1) * plane] for g in range(len(groups))]


def unpack_kernel(plane, chunk0, chunks, count, place_ref, *refs):
    ins, (out, held, sem_in, sem_out) = refs[:count * plane], refs[-4:]
    place = place_ref[0]
    width = plane * LANES
    at, loads = 0, []
    for group in range(count):
        for chunk in range(ins[group * plane].shape[0]):
            for k in range(plane):
                copy = pltpu.make_async_copy(
                    ins[group * plane + k].at[chunk],
                    held.at[at, :, columns(place ^ k, 0, plane)],
                    sem_in.at[at, k],
                )
                copy.start()
                loads.append(copy)
            at += 1
    stores = []
    for at in range(chunks):
        for copy in loads[at * plane:(at + 1) * plane]:
            copy.wait()
        copy = pltpu.make_async_copy(
            held.at[at], out.at[:, pl.ds((chunk0 + at) * width, width)], sem_out.at[at]
        )
        copy.start()
        stores.append(copy)
    for copy in stores:
        copy.wait()


def unpack(place, groups, chunk0, total, into):
    plane = len(groups[0])
    chunks = sum(g[0].shape[0] for g in groups)
    _, rows, _ = groups[0][0].shape
    dtype = groups[0][0].dtype
    flat = [x for g in groups for x in g]
    extra = [] if into is None else [into]
    return pl.pallas_call(
        functools.partial(unpack_kernel, plane, chunk0, chunks, len(groups)),
        in_specs=[SMEM] + [ANY] * (len(flat) + len(extra)),
        out_specs=ANY,
        out_shape=jax.ShapeDtypeStruct((rows, total * plane * LANES), dtype),
        scratch_shapes=[
            pltpu.VMEM((chunks, rows, plane * LANES), dtype),
            pltpu.SemaphoreType.DMA((chunks, plane)),
            pltpu.SemaphoreType.DMA((chunks,)),
        ],
        input_output_aliases={} if into is None else {1 + len(flat): 0},
        cost_estimate=pl.CostEstimate(
            flops=0, bytes_accessed=chunks * rows * plane * LANES * 4, transcendentals=0
        ),
        compiler_params=PARAMS,
    )(place, *flat, *extra)


def scores(query, tiles, slope, store):
    best = None
    for at, (keys, _, bias) in enumerate(tiles):
        tile = lax.dot_general(
            query, keys[...], (((1,), (1,)), ((), ())), preferred_element_type=jnp.float32
        )
        tile = tile + slope * bias[...]
        store[at] = tile
        for lane in range(0, tile.shape[1], LANES):
            part = tile[:, lane:lane + LANES]
            best = part if best is None else jnp.maximum(best, part)
    return jnp.broadcast_to(jnp.max(best, axis=1, keepdims=True), best.shape)


def weigh(tiles, peak, store, dtype):
    acc = None
    for at, (_, values, _) in enumerate(tiles):
        raised = jnp.concatenate(
            [
                jnp.exp(store[at, :, lane:lane + LANES] - peak).astype(dtype)
                for lane in range(0, store.shape[2], LANES)
            ],
            axis=1,
        )
        part = jnp.dot(raised, values[...], preferred_element_type=jnp.float32)
        acc = part if acc is None else acc + part
    return acc


def lanes_of(head_width, head):
    return lax.broadcasted_iota(jnp.int32, (1, LANES), 1) // head_width == head


def near_kernel(win, plane, chunk0, head_width, place_ref, slopes, *refs):
    qs = refs[:plane]
    uks, uvs = refs[plane:2 * plane], refs[2 * plane:3 * plane]
    oks, ovs = refs[3 * plane:4 * plane], refs[4 * plane:5 * plane]
    bias, acc_ref, peak_ref, store, keys, ones, query = refs[5 * plane:]
    place = place_ref[0]
    heads = LANES // head_width
    chunk, head = pl.program_id(0) + chunk0, pl.program_id(1)
    dtype = keys.dtype
    slope = slopes[(chunk * plane + place) * heads + head]
    mine = lanes_of(head_width, head)
    scale = jnp.asarray(head_width ** -0.5, dtype)
    for k in range(plane):
        at = place ^ k
        query[at] = jnp.where(mine, qs[k][0] * scale, jnp.zeros((), dtype))
        ones[at] = jnp.where(mine, uvs[k][0], jnp.ones((), dtype))
        ones[plane + at] = jnp.where(mine, ovs[k][0], jnp.ones((), dtype))
        keys[at] = uks[k][0]
        keys[plane + at] = oks[k][0]
    for i in range(plane):
        tiles = []
        for b in range(2 * plane):
            offset = b - plane - i
            if offset >= -win:
                tiles.append((keys.at[b], ones.at[b], bias.at[offset + win]))
        slot = store.at[i % 2]
        peak = scores(query[i], tiles, slope, slot)
        peak_ref[0, 0, i] = peak
        acc_ref[0, 0, i] = weigh(tiles, peak, slot, dtype)


def near(place, slopes, qs, ups, owns, bias, chunk0, chunks, head_width):
    plane = len(qs)
    _, rows, _ = qs[0].shape
    win = bias.shape[0] // 2
    heads = LANES // head_width
    block = (1, rows, LANES)
    pairs = chunks * heads * rows * rows * (plane * plane + plane * (plane + 1) // 2)
    key_spec = pl.BlockSpec(block, lambda c, h: (c, 0, 0))
    value_spec = pl.BlockSpec(block, lambda c, h: (chunks + c, 0, 0))
    query_spec = pl.BlockSpec(block, lambda c, h: (chunk0 + c, 0, 0))
    out = (chunks, heads, plane, rows, LANES)
    out_spec = pl.BlockSpec((1, 1) + out[2:], lambda c, h: (c, h, 0, 0, 0))
    return pl.pallas_call(
        functools.partial(near_kernel, win, plane, chunk0, head_width),
        grid=(chunks, heads),
        in_specs=[SMEM, SMEM] + [query_spec] * plane + [key_spec] * plane + [value_spec] * plane
        + [key_spec] * plane + [value_spec] * plane
        + [pl.BlockSpec(bias.shape, lambda c, h: (0, 0, 0), pipeline_mode=pl.Buffered(1))],
        out_specs=[out_spec, out_spec],
        out_shape=[jax.ShapeDtypeStruct(out, jnp.float32)] * 2,
        scratch_shapes=[
            pltpu.VMEM((2, 2 * win, rows, rows), jnp.float32),
            pltpu.VMEM((2 * plane, rows, LANES), qs[0].dtype),
            pltpu.VMEM((2 * plane, rows, LANES), qs[0].dtype),
            pltpu.VMEM((plane, rows, LANES), qs[0].dtype),
        ],
        cost_estimate=pl.CostEstimate(
            flops=4 * pairs * LANES, bytes_accessed=chunks * (4 << 20), transcendentals=pairs
        ),
        compiler_params=PARAMS,
        name="near",
    )(place, slopes, *qs, *ups, *ups, *owns, *owns, bias)


def far_kernel(win, plane, chunk0, head_width, place_ref, slopes, *refs):
    qs, dks, dvs = (refs[n * plane:(n + 1) * plane] for n in range(3))
    bias, acc_ref, peak_ref = refs[3 * plane:3 * plane + 3]
    outs = refs[3 * plane + 3:4 * plane + 3]
    store, keys, ones, query, held = refs[4 * plane + 3:]
    place = place_ref[0]
    heads = LANES // head_width
    chunk = pl.program_id(0) + chunk0
    dtype = keys.dtype
    scale = jnp.asarray(head_width ** -0.5, dtype)
    for k in range(plane):
        at = place ^ k
        keys[at] = dks[k][0]
        for head in range(heads):
            mine = lanes_of(head_width, head)
            query[head, at] = jnp.where(mine, qs[k][0] * scale, jnp.zeros((), dtype))
            ones[head, at] = jnp.where(mine, dvs[k][0], jnp.ones((), dtype))
    for i in range(plane):
        upper = lower = None
        for head in range(heads):
            slope = slopes[(chunk * plane + place) * heads + head]
            tiles = [
                (keys.at[b], ones.at[head, b], bias.at[b + plane - i - 1])
                for b in range(plane) if b + plane - i <= win
            ]
            slot = store.at[(i * heads + head) % store.shape[0]]
            before = peak_ref[0, head, i]
            peak = jnp.maximum(scores(query[head, i], tiles, slope, slot), before)
            acc = weigh(tiles, peak, slot, dtype) + acc_ref[0, head, i] * jnp.exp(before - peak)
            if upper is None:
                upper, lower = acc, acc
            else:
                mine = lanes_of(head_width, head)
                beside = lanes_of(head_width, head - 1)
                upper = jnp.where(mine, acc, upper)
                lower = jnp.where(beside, acc, lower)
        lower = pltpu.roll(lower, head_width, 1)
        held[i ^ place] = (upper / lower).astype(dtype)
    for k in range(plane):
        outs[k][0] = held[k]


def far(place, slopes, qs, downs, bias, before, chunk0, chunks, head_width):
    plane = len(qs)
    _, rows, _ = qs[0].shape
    win = bias.shape[0]
    heads = LANES // head_width
    block = (1, rows, LANES)
    pairs = chunks * heads * rows * rows * (plane * (plane + 1) // 2)
    acc, peak = before
    key_spec = pl.BlockSpec(block, lambda c: (c, 0, 0))
    value_spec = pl.BlockSpec(block, lambda c: (chunks + c, 0, 0))
    query_spec = pl.BlockSpec(block, lambda c: (chunk0 + c, 0, 0))
    near_spec = pl.BlockSpec(
        (1, heads, plane, rows, LANES), lambda c: (c, 0, 0, 0, 0)
    )
    return pl.pallas_call(
        functools.partial(far_kernel, win, plane, chunk0, head_width),
        grid=(chunks,),
        in_specs=[SMEM, SMEM] + [query_spec] * plane + [key_spec] * plane + [value_spec] * plane
        + [pl.BlockSpec(bias.shape, lambda c: (0, 0, 0), pipeline_mode=pl.Buffered(1))]
        + [near_spec, near_spec],
        out_specs=[key_spec] * plane,
        out_shape=[jax.ShapeDtypeStruct((chunks, rows, LANES), qs[0].dtype)] * plane,
        scratch_shapes=[
            pltpu.VMEM((2 * heads, win, rows, rows), jnp.float32),
            pltpu.VMEM((plane, rows, LANES), qs[0].dtype),
            pltpu.VMEM((heads, plane, rows, LANES), qs[0].dtype),
            pltpu.VMEM((heads, plane, rows, LANES), qs[0].dtype),
            pltpu.VMEM((plane, rows, LANES), qs[0].dtype),
        ],
        cost_estimate=pl.CostEstimate(
            flops=4 * pairs * LANES, bytes_accessed=chunks * (4 << 20), transcendentals=pairs
        ),
        compiler_params=PARAMS,
        name="far",
    )(place, slopes, *qs, *downs, *downs, bias, acc, peak)


def per_device(queries, key_rows, values, bias_tiles, buckets, slopes):
    count = lax.axis_size("seq")
    plane = buckets.shape[0] - 1
    width = queries.shape[1]
    head_width = width // slopes.shape[0]
    chunks = width // (plane * LANES)

    def send(arrays):
        out = list(arrays[:1])
        for k, x in enumerate(arrays[1:], 1):
            pairs = [(i, i ^ k) for i in range(count)]
            out.append(lax.ppermute(x, "seq", pairs))
        return out

    def shift(arrays, step):
        pairs = [(i, (i + step * plane) % count) for i in range(count)]
        return [lax.ppermute(x, "seq", pairs) for x in arrays]

    place = (lax.axis_index("seq") % plane).astype(jnp.int32).reshape(1)
    data = dict(q=queries, k=key_rows, v=values)

    def kv(start, size):
        span = range(start, start + size)
        return [("k", c) for c in span] + [("v", c) for c in span]

    groups = [(0, chunks - 1), (chunks - 1, 1)]
    (first,) = pack(dict(k=key_rows, v=values), [kv(*groups[0])], plane, place)
    second, query = pack(data, [kv(*groups[1]), [("q", c) for c in range(chunks)]], plane, place)
    owns = [send(x) for x in (first, second)]
    qs = send(query)
    near_bias, far_bias = bias_window(bias_tiles, buckets)
    ups = [shift(x, 1) for x in owns]
    downs = [shift(x, -1) for x in owns]
    sums, back = [], []
    for g, (start, size) in enumerate(groups):
        sums.append(near(place, slopes, qs, ups[g], owns[g], near_bias, start, size, head_width))
    for g, (start, size) in enumerate(groups):
        outs = far(place, slopes, qs, downs[g], far_bias, sums[g], start, size, head_width)
        back.append(send(outs))
    most = unpack(place, back[:1], 0, chunks, None)
    return unpack(place, back[1:], chunks - 1, chunks, most)


def solution(mesh):
    rows = P(("batch", "seq"), None)
    return jax.shard_map(
        per_device,
        mesh=mesh,
        in_specs=(rows, rows, rows, P(), P(), P()),
        out_specs=rows,
        check_vma=False,
    )
```

```python
import functools

import jax
import jax.numpy as jnp
from jax import lax
from jax.experimental import pallas as pl
from jax.experimental.pallas import tpu as pltpu
from jax.sharding import PartitionSpec as P


LANES = 128
FULL = 67043328
ANY = pl.BlockSpec(memory_space=pl.ANY)
SMEM = pl.BlockSpec(memory_space=pltpu.SMEM)
PARAMS = pltpu.CompilerParams(vmem_limit_bytes=FULL)


def bias_kernel(win, buckets, tile_ref, near_ref, far_ref):
    for t in range(-win, win + 1):
        tile = tile_ref[buckets[abs(t)]].astype(jnp.float32)
        if t < win:
            near_ref[t + win] = tile if t < 0 else tile.T
        if t > 0:
            far_ref[t - 1] = tile.T


def bias_window(bias_tiles, buckets):
    win = buckets.shape[0] - 1
    side = bias_tiles.shape[1]
    vmem = pl.BlockSpec(memory_space=pltpu.VMEM)
    return pl.pallas_call(
        functools.partial(bias_kernel, win),
        in_specs=[SMEM, vmem],
        out_specs=[vmem, vmem],
        out_shape=[
            jax.ShapeDtypeStruct((2 * win, side, side), jnp.float32),
            jax.ShapeDtypeStruct((win, side, side), jnp.float32),
        ],
        compiler_params=PARAMS,
        name="bias_window",
    )(buckets, bias_tiles)


def columns(place, chunk, plane):
    return pl.ds(pl.multiple_of((place + chunk * plane) * LANES, LANES), LANES)


def pack_kernel(plane, groups, names, place_ref, *refs):
    ins, outs = refs[:len(names)], refs[len(names):-3]
    held, sem_in, sem_out = refs[-3:]
    place = place_ref[0]
    width = plane * LANES
    slots = sorted({item for group in groups for item in group})
    loads, stores = {}, []
    for at, (array, chunk) in enumerate(slots):
        loads[array, chunk] = copy = pltpu.make_async_copy(
            ins[names.index(array)].at[:, pl.ds(chunk * width, width)], held.at[at], sem_in.at[at]
        )
        copy.start()
    waited = set()
    for g, group in enumerate(groups):
        for slot, item in enumerate(group):
            if item not in waited:
                loads[item].wait()
                waited.add(item)
            for k in range(plane):
                copy = pltpu.make_async_copy(
                    held.at[slots.index(item), :, columns(place ^ k, 0, plane)],
                    outs[g * plane + k].at[slot],
                    sem_out.at[len(stores)],
                )
                copy.start()
                stores.append(copy)
    for copy in stores:
        copy.wait()


def pack(arrays, groups, plane, place):
    names = list(arrays)
    first = arrays[names[0]]
    rows = first.shape[0]
    slots = len({item for g in groups for item in g})
    stores = plane * sum(len(g) for g in groups)
    outs = pl.pallas_call(
        functools.partial(pack_kernel, plane, groups, names),
        in_specs=[SMEM] + [ANY] * len(names),
        out_specs=[ANY] * (plane * len(groups)),
        out_shape=[
            jax.ShapeDtypeStruct((len(g), rows, LANES), first.dtype)
            for g in groups for _ in range(plane)
        ],
        scratch_shapes=[
            pltpu.VMEM((slots, rows, plane * LANES), first.dtype),
            pltpu.SemaphoreType.DMA((slots,)),
            pltpu.SemaphoreType.DMA((stores,)),
        ],
        cost_estimate=pl.CostEstimate(
            flops=0, bytes_accessed=stores * rows * LANES * 4, transcendentals=0
        ),
        compiler_params=PARAMS,
    )(place, *arrays.values())
    return [outs[g * plane:(g + 1) * plane] for g in range(len(groups))]


def unpack_kernel(plane, chunk0, chunks, count, place_ref, *refs):
    ins, (out, held, sem_in, sem_out) = refs[:count * plane], refs[-4:]
    place = place_ref[0]
    width = plane * LANES
    at, loads = 0, []
    for group in range(count):
        for chunk in range(ins[group * plane].shape[0]):
            for k in range(plane):
                copy = pltpu.make_async_copy(
                    ins[group * plane + k].at[chunk],
                    held.at[at, :, columns(place ^ k, 0, plane)],
                    sem_in.at[at, k],
                )
                copy.start()
                loads.append(copy)
            at += 1
    stores = []
    for at in range(chunks):
        for copy in loads[at * plane:(at + 1) * plane]:
            copy.wait()
        copy = pltpu.make_async_copy(
            held.at[at], out.at[:, pl.ds((chunk0 + at) * width, width)], sem_out.at[at]
        )
        copy.start()
        stores.append(copy)
    for copy in stores:
        copy.wait()


def unpack(place, groups, chunk0, total, into):
    plane = len(groups[0])
    chunks = sum(g[0].shape[0] for g in groups)
    _, rows, _ = groups[0][0].shape
    dtype = groups[0][0].dtype
    flat = [x for g in groups for x in g]
    extra = [] if into is None else [into]
    return pl.pallas_call(
        functools.partial(unpack_kernel, plane, chunk0, chunks, len(groups)),
        in_specs=[SMEM] + [ANY] * (len(flat) + len(extra)),
        out_specs=ANY,
        out_shape=jax.ShapeDtypeStruct((rows, total * plane * LANES), dtype),
        scratch_shapes=[
            pltpu.VMEM((chunks, rows, plane * LANES), dtype),
            pltpu.SemaphoreType.DMA((chunks, plane)),
            pltpu.SemaphoreType.DMA((chunks,)),
        ],
        input_output_aliases={} if into is None else {1 + len(flat): 0},
        cost_estimate=pl.CostEstimate(
            flops=0, bytes_accessed=chunks * rows * plane * LANES * 4, transcendentals=0
        ),
        compiler_params=PARAMS,
    )(place, *flat, *extra)


LOG2E = 1.4426950408889634


SUB = 8


def attend(query, keys, bias, store):
    rows = query.shape[0]
    best = None
    for t, tile_bias in enumerate(bias):
        tile = lax.dot_general(
            keys[pl.ds(t * rows, rows), :], query, (((1,), (1,)), ((), ())),
            preferred_element_type=jnp.float32,
        )
        tile = tile * LOG2E + tile_bias[...]
        store[pl.ds(t * rows, rows), :] = tile
        part = jnp.max(tile.reshape(rows // SUB, SUB, rows), axis=0)
        best = part if best is None else jnp.maximum(best, part)
    return jnp.broadcast_to(jnp.max(best, axis=0, keepdims=True), best.shape)


def weigh(values, peak, count, store):
    rows = store.shape[1]
    acc = None
    for t in range(count):
        tile = store[pl.ds(t * rows, rows), :].reshape(rows // SUB, SUB, rows)
        raised = jnp.exp2(tile - peak[None]).reshape(rows, rows).astype(values.dtype)
        part = jnp.dot(
            values[:, pl.ds(t * rows, rows)], raised, preferred_element_type=jnp.float32
        )
        acc = part if acc is None else acc + part
    return acc


def lanes_of(head_width, head):
    return lax.broadcasted_iota(jnp.int32, (1, LANES), 1) // head_width == head


def turned(values, head, head_width):
    flat = values.astype(jnp.float32).T
    return flat[head * head_width:(head + 1) * head_width].astype(values.dtype)


def near_kernel(win, plane, chunk0, head_width, place_ref, slopes, *refs):
    qs = refs[:plane]
    uks, uvs = refs[plane:2 * plane], refs[2 * plane:3 * plane]
    oks, ovs = refs[3 * plane:4 * plane], refs[4 * plane:5 * plane]
    bias, out_ref, store, keys, flat, query, scaled = refs[5 * plane:]
    place = place_ref[0]
    heads = LANES // head_width
    chunk = pl.program_id(0) + chunk0
    dtype = keys.dtype
    rows = query.shape[2]
    scale = jnp.asarray(head_width ** -0.5, dtype)
    for k in range(plane):
        at = place ^ k
        for base, ks, vs in ((0, uks, uvs), (plane, oks, ovs)):
            span = pl.ds(pl.multiple_of((base + at) * rows, rows), rows)
            keys[span, :] = ks[k][0]
            for head in range(heads):
                flat[head, :head_width, span] = turned(vs[k][0], head, head_width)
        for head in range(heads):
            query[head, at] = jnp.where(
                lanes_of(head_width, head), qs[k][0] * scale, jnp.zeros((), dtype)
            )
    for head in range(heads):
        flat[head, head_width:, :] = jnp.ones((2 * SUB, flat.shape[2]), dtype)

    def one(head, _):
        slope = slopes[(chunk * plane + place) * heads + head] * LOG2E
        for t in range(2 * win):
            scaled[t] = bias[t] * slope
        for i in range(plane):
            first = max(0, i + plane - win)
            count = 2 * plane - first
            tiles = [scaled.at[b - plane - i + win] for b in range(first, 2 * plane)]
            span = pl.ds(first * rows, count * rows)
            peak = attend(query[head, i], keys.at[span], tiles, store.at[i % 2])
            acc = weigh(flat.at[head, :, span], peak, count, store.at[i % 2])
            out_ref[0, head, i, :head_width + SUB] = acc[:head_width + SUB]
            out_ref[0, head, i, head_width + SUB:] = peak
        return 0

    lax.fori_loop(0, heads, one, 0)


def near(place, slopes, qs, ups, owns, bias, chunk0, chunks, head_width):
    plane = len(qs)
    _, rows, _ = qs[0].shape
    win = bias.shape[0] // 2
    heads = LANES // head_width
    block = (1, rows, LANES)
    pairs = chunks * heads * rows * rows * (plane * plane + plane * (plane + 1) // 2)
    key_spec = pl.BlockSpec(block, lambda c: (c, 0, 0))
    value_spec = pl.BlockSpec(block, lambda c: (chunks + c, 0, 0))
    query_spec = pl.BlockSpec(block, lambda c: (chunk0 + c, 0, 0))
    out = (chunks, heads, plane, head_width + 2 * SUB, rows)
    dtype = qs[0].dtype
    return pl.pallas_call(
        functools.partial(near_kernel, win, plane, chunk0, head_width),
        grid=(chunks,),
        in_specs=[SMEM, SMEM] + [query_spec] * plane + [key_spec] * plane + [value_spec] * plane
        + [key_spec] * plane + [value_spec] * plane
        + [pl.BlockSpec(bias.shape, lambda c: (0, 0, 0), pipeline_mode=pl.Buffered(1))],
        out_specs=pl.BlockSpec((1,) + out[1:], lambda c: (c, 0, 0, 0, 0)),
        out_shape=jax.ShapeDtypeStruct(out, jnp.float32),
        scratch_shapes=[
            pltpu.VMEM((2, 2 * win * rows, rows), jnp.float32),
            pltpu.VMEM((2 * plane * rows, LANES), dtype),
            pltpu.VMEM((heads, head_width + 2 * SUB, 2 * plane * rows), dtype),
            pltpu.VMEM((heads, plane, rows, LANES), dtype),
            pltpu.VMEM((2 * win, rows, rows), jnp.float32),
        ],
        cost_estimate=pl.CostEstimate(
            flops=4 * pairs * LANES, bytes_accessed=chunks * (4 << 20), transcendentals=pairs
        ),
        compiler_params=PARAMS,
        name="near",
    )(place, slopes, *qs, *ups, *ups, *owns, *owns, bias)


def far_kernel(win, plane, chunk0, head_width, place_ref, slopes, *refs):
    qs, dks, dvs = (refs[n * plane:(n + 1) * plane] for n in range(3))
    bias, near_ref = refs[3 * plane:3 * plane + 2]
    outs = refs[3 * plane + 2:4 * plane + 2]
    store, keys, flat, query, held, scaled = refs[4 * plane + 2:]
    place = place_ref[0]
    heads = LANES // head_width
    chunk = pl.program_id(0) + chunk0
    dtype = keys.dtype
    rows = query.shape[2]
    scale = jnp.asarray(head_width ** -0.5, dtype)
    for k in range(plane):
        at = place ^ k
        span = pl.ds(pl.multiple_of(at * rows, rows), rows)
        keys[span, :] = dks[k][0]
        for head in range(heads):
            flat[head, :head_width, span] = turned(dvs[k][0], head, head_width)
            query[head, at] = jnp.where(
                lanes_of(head_width, head), qs[k][0] * scale, jnp.zeros((), dtype)
            )
    for head in range(heads):
        flat[head, head_width:, :] = jnp.ones((2 * SUB, flat.shape[2]), dtype)
        slope = slopes[(chunk * plane + place) * heads + head] * LOG2E
        for t in range(win):
            scaled[head, t] = bias[t] * slope
    for i in range(plane):
        count = min(plane, win - plane + i + 1)
        span = pl.ds(0, count * rows)
        both = []
        for head in range(heads):
            tiles = [scaled.at[head, b + plane - i - 1] for b in range(count)]
            slot = store.at[(i * heads + head) % 2]
            before = near_ref[0, head, i, head_width + SUB:]
            peak = jnp.maximum(attend(query[head, i], keys.at[span], tiles, slot), before)
            acc = weigh(flat.at[head, :, span], peak, count, slot)[:head_width + SUB]
            acc = acc.reshape(-1, SUB, rows)
            old = near_ref[0, head, i, :head_width + SUB].reshape(-1, SUB, rows)
            acc = acc + old * jnp.exp2(before - peak)[None]
            share = 1.0 / acc[head_width // SUB:]
            both.append((acc[:head_width // SUB] * share).reshape(head_width, rows))
        held[i ^ place] = jnp.concatenate(both, axis=0).T.astype(dtype)
    for k in range(plane):
        outs[k][0] = held[k]


def far(place, slopes, qs, downs, bias, before, chunk0, chunks, head_width):
    plane = len(qs)
    _, rows, _ = qs[0].shape
    win = bias.shape[0]
    heads = LANES // head_width
    block = (1, rows, LANES)
    pairs = chunks * heads * rows * rows * (plane * (plane + 1) // 2)
    key_spec = pl.BlockSpec(block, lambda c: (c, 0, 0))
    value_spec = pl.BlockSpec(block, lambda c: (chunks + c, 0, 0))
    query_spec = pl.BlockSpec(block, lambda c: (chunk0 + c, 0, 0))
    near_spec = pl.BlockSpec((1,) + before.shape[1:], lambda c: (c, 0, 0, 0, 0))
    dtype = qs[0].dtype
    return pl.pallas_call(
        functools.partial(far_kernel, win, plane, chunk0, head_width),
        grid=(chunks,),
        in_specs=[SMEM, SMEM] + [query_spec] * plane + [key_spec] * plane + [value_spec] * plane
        + [pl.BlockSpec(bias.shape, lambda c: (0, 0, 0), pipeline_mode=pl.Buffered(1))]
        + [near_spec],
        out_specs=[key_spec] * plane,
        out_shape=[jax.ShapeDtypeStruct((chunks, rows, LANES), dtype)] * plane,
        scratch_shapes=[
            pltpu.VMEM((2, plane * rows, rows), jnp.float32),
            pltpu.VMEM((plane * rows, LANES), dtype),
            pltpu.VMEM((heads, head_width + 2 * SUB, plane * rows), dtype),
            pltpu.VMEM((heads, plane, rows, LANES), dtype),
            pltpu.VMEM((plane, rows, LANES), dtype),
            pltpu.VMEM((heads, win, rows, rows), jnp.float32),
        ],
        cost_estimate=pl.CostEstimate(
            flops=4 * pairs * LANES, bytes_accessed=chunks * (4 << 20), transcendentals=pairs
        ),
        compiler_params=PARAMS,
        name="far",
    )(place, slopes, *qs, *downs, *downs, bias, before)


def per_device(queries, key_rows, values, bias_tiles, buckets, slopes):
    count = lax.axis_size("seq")
    plane = buckets.shape[0] - 1
    width = queries.shape[1]
    head_width = width // slopes.shape[0]
    chunks = width // (plane * LANES)

    def send(arrays):
        out = list(arrays[:1])
        for k, x in enumerate(arrays[1:], 1):
            pairs = [(i, i ^ k) for i in range(count)]
            out.append(lax.ppermute(x, "seq", pairs))
        return out

    def shift(arrays, step):
        pairs = [(i, (i + step * plane) % count) for i in range(count)]
        return [lax.ppermute(x, "seq", pairs) for x in arrays]

    place = (lax.axis_index("seq") % plane).astype(jnp.int32).reshape(1)

    def kv(start, size):
        span = range(start, start + size)
        return [("k", c) for c in span] + [("v", c) for c in span]

    groups = [(0, chunks - 1), (chunks - 1, 1)]
    first, second = pack(dict(k=key_rows, v=values), [kv(*g) for g in groups], plane, place)
    (query,) = pack(dict(q=queries), [[("q", c) for c in range(chunks)]], plane, place)
    owns = [send(x) for x in (first, second)]
    qs = send(query)
    near_bias, far_bias = bias_window(bias_tiles, buckets)
    ups = [shift(x, 1) for x in owns]
    downs = [shift(x, -1) for x in owns]
    sums, back = [], []
    for g, (start, size) in enumerate(groups):
        sums.append(near(place, slopes, qs, ups[g], owns[g], near_bias, start, size, head_width))
    for g, (start, size) in enumerate(groups):
        outs = far(place, slopes, qs, downs[g], far_bias, sums[g], start, size, head_width)
        back.append(send(outs))
    most = unpack(place, back[:1], 0, chunks, None)
    return unpack(place, back[1:], chunks - 1, chunks, most)


def solution(mesh):
    rows = P(("batch", "seq"), None)
    return jax.shard_map(
        per_device,
        mesh=mesh,
        in_specs=(rows, rows, rows, P(), P(), P()),
        out_specs=rows,
        check_vma=False,
    )
```

```python
import functools

import jax
import jax.numpy as jnp
from jax import lax
from jax.experimental import pallas as pl
from jax.experimental.pallas import tpu as pltpu
from jax.sharding import PartitionSpec as P


LANES = 128
FULL = 67043328
ANY = pl.BlockSpec(memory_space=pl.ANY)
SMEM = pl.BlockSpec(memory_space=pltpu.SMEM)
PARAMS = pltpu.CompilerParams(vmem_limit_bytes=FULL)


def bias_kernel(win, buckets, tile_ref, near_ref, far_ref):
    for t in range(-win, win + 1):
        tile = tile_ref[buckets[abs(t)]].astype(jnp.float32)
        if t < win:
            near_ref[t + win] = tile if t < 0 else tile.T
        if t > 0:
            far_ref[t - 1] = tile.T


def bias_window(bias_tiles, buckets):
    win = buckets.shape[0] - 1
    side = bias_tiles.shape[1]
    vmem = pl.BlockSpec(memory_space=pltpu.VMEM)
    return pl.pallas_call(
        functools.partial(bias_kernel, win),
        in_specs=[SMEM, vmem],
        out_specs=[vmem, vmem],
        out_shape=[
            jax.ShapeDtypeStruct((2 * win, side, side), jnp.float32),
            jax.ShapeDtypeStruct((win, side, side), jnp.float32),
        ],
        compiler_params=PARAMS,
        name="bias_window",
    )(buckets, bias_tiles)


def columns(place, chunk, plane):
    return pl.ds(pl.multiple_of((place + chunk * plane) * LANES, LANES), LANES)


def pack_kernel(plane, groups, names, place_ref, *refs):
    ins, outs = refs[:len(names)], refs[len(names):-3]
    held, sem_in, sem_out = refs[-3:]
    place = place_ref[0]
    width = plane * LANES
    slots = sorted({item for group in groups for item in group})
    loads, stores = {}, []
    for at, (array, chunk) in enumerate(slots):
        loads[array, chunk] = copy = pltpu.make_async_copy(
            ins[names.index(array)].at[:, pl.ds(chunk * width, width)], held.at[at], sem_in.at[at]
        )
        copy.start()
    waited = set()
    for g, group in enumerate(groups):
        for slot, item in enumerate(group):
            if item not in waited:
                loads[item].wait()
                waited.add(item)
            for k in range(plane):
                copy = pltpu.make_async_copy(
                    held.at[slots.index(item), :, columns(place ^ k, 0, plane)],
                    outs[g * plane + k].at[slot],
                    sem_out.at[len(stores)],
                )
                copy.start()
                stores.append(copy)
    for copy in stores:
        copy.wait()


def pack(arrays, groups, plane, place):
    names = list(arrays)
    first = arrays[names[0]]
    rows = first.shape[0]
    slots = len({item for g in groups for item in g})
    stores = plane * sum(len(g) for g in groups)
    outs = pl.pallas_call(
        functools.partial(pack_kernel, plane, groups, names),
        in_specs=[SMEM] + [ANY] * len(names),
        out_specs=[ANY] * (plane * len(groups)),
        out_shape=[
            jax.ShapeDtypeStruct((len(g), rows, LANES), first.dtype)
            for g in groups for _ in range(plane)
        ],
        scratch_shapes=[
            pltpu.VMEM((slots, rows, plane * LANES), first.dtype),
            pltpu.SemaphoreType.DMA((slots,)),
            pltpu.SemaphoreType.DMA((stores,)),
        ],
        cost_estimate=pl.CostEstimate(
            flops=0, bytes_accessed=stores * rows * LANES * 4, transcendentals=0
        ),
        compiler_params=PARAMS,
    )(place, *arrays.values())
    return [outs[g * plane:(g + 1) * plane] for g in range(len(groups))]


def unpack_kernel(plane, chunk0, chunks, count, place_ref, *refs):
    ins, (out, held, sem_in, sem_out) = refs[:count * plane], refs[-4:]
    place = place_ref[0]
    width = plane * LANES
    at, loads = 0, []
    for group in range(count):
        for chunk in range(ins[group * plane].shape[0]):
            for k in range(plane):
                copy = pltpu.make_async_copy(
                    ins[group * plane + k].at[chunk],
                    held.at[at, :, columns(place ^ k, 0, plane)],
                    sem_in.at[at, k],
                )
                copy.start()
                loads.append(copy)
            at += 1
    stores = []
    for at in range(chunks):
        for copy in loads[at * plane:(at + 1) * plane]:
            copy.wait()
        copy = pltpu.make_async_copy(
            held.at[at], out.at[:, pl.ds((chunk0 + at) * width, width)], sem_out.at[at]
        )
        copy.start()
        stores.append(copy)
    for copy in stores:
        copy.wait()


def unpack(place, groups, chunk0, total, into):
    plane = len(groups[0])
    chunks = sum(g[0].shape[0] for g in groups)
    _, rows, _ = groups[0][0].shape
    dtype = groups[0][0].dtype
    flat = [x for g in groups for x in g]
    extra = [] if into is None else [into]
    return pl.pallas_call(
        functools.partial(unpack_kernel, plane, chunk0, chunks, len(groups)),
        in_specs=[SMEM] + [ANY] * (len(flat) + len(extra)),
        out_specs=ANY,
        out_shape=jax.ShapeDtypeStruct((rows, total * plane * LANES), dtype),
        scratch_shapes=[
            pltpu.VMEM((chunks, rows, plane * LANES), dtype),
            pltpu.SemaphoreType.DMA((chunks, plane)),
            pltpu.SemaphoreType.DMA((chunks,)),
        ],
        input_output_aliases={} if into is None else {1 + len(flat): 0},
        cost_estimate=pl.CostEstimate(
            flops=0, bytes_accessed=chunks * rows * plane * LANES * 4, transcendentals=0
        ),
        compiler_params=PARAMS,
    )(place, *flat, *extra)


LOG2E = 1.4426950408889634


SUB = 8


class Block:
    def __init__(self, query, keys, values, bias, store, piece):
        self.query, self.keys, self.values, self.bias, self.store = query, keys, values, bias, store
        rows, self.piece = query.shape[0], piece
        self.pieces = [
            (t, at) for t in range(len(bias)) for at in range(0, rows, piece)
        ]
        self.rows, self.best, self.acc, self.floor = rows, None, None, None

    def score(self, n):
        t, at = self.pieces[n]
        start = t * self.rows + at
        tile = lax.dot_general(
            self.keys[pl.ds(start, self.piece), :], self.query, (((1,), (1,)), ((), ())),
            preferred_element_type=jnp.float32,
        )
        tile = tile * LOG2E + self.bias[t][pl.ds(at, self.piece), :]
        self.store[pl.ds(start, self.piece), :] = tile
        part = jnp.max(tile.reshape(self.piece // SUB, SUB, self.rows), axis=0)
        self.best = part if self.best is None else jnp.maximum(self.best, part)

    def close(self):
        peak = jnp.broadcast_to(jnp.max(self.best, axis=0, keepdims=True), self.best.shape)
        self.peak = peak if self.floor is None else jnp.maximum(peak, self.floor)

    def weigh(self, n):
        t, at = self.pieces[n]
        start = t * self.rows + at
        tile = self.store[pl.ds(start, self.piece), :].reshape(self.piece // SUB, SUB, self.rows)
        raised = jnp.exp2(tile - self.peak[None]).reshape(self.piece, self.rows)
        part = jnp.dot(
            self.values[:, pl.ds(start, self.piece)], raised.astype(self.keys.dtype),
            preferred_element_type=jnp.float32,
        )
        self.acc = part if self.acc is None else self.acc + part


def pipeline(blocks, finish):
    before = None
    for block in list(blocks) + [None]:
        ahead = len(block.pieces) if block is not None else 0
        behind = len(before.pieces) if before is not None else 0
        most = max(ahead, behind)
        done = [0, 0]
        for n in range(most):
            for which, count, run in (
                (0, behind, before.weigh if before is not None else None),
                (1, ahead, block.score if block is not None else None),
            ):
                while done[which] * most < count * (n + 1):
                    run(done[which])
                    done[which] += 1
        if block is not None:
            block.close()
        if before is not None:
            finish(before)
        before = block


def lanes_of(head_width, head):
    return lax.broadcasted_iota(jnp.int32, (1, LANES), 1) // head_width == head


def turned(values, head, head_width):
    flat = values.astype(jnp.float32).T
    return flat[head * head_width:(head + 1) * head_width].astype(values.dtype)


def near_kernel(win, plane, chunk0, head_width, place_ref, slopes, *refs):
    qs = refs[:plane]
    uks, uvs = refs[plane:2 * plane], refs[2 * plane:3 * plane]
    oks, ovs = refs[3 * plane:4 * plane], refs[4 * plane:5 * plane]
    bias, out_ref, store, keys, flat, query, scaled = refs[5 * plane:]
    place = place_ref[0]
    heads = LANES // head_width
    chunk = pl.program_id(0) + chunk0
    dtype = keys.dtype
    rows = query.shape[2]
    scale = jnp.asarray(head_width ** -0.5, dtype)
    for k in range(plane):
        at = place ^ k
        for base, ks, vs in ((0, uks, uvs), (plane, oks, ovs)):
            span = pl.ds(pl.multiple_of((base + at) * rows, rows), rows)
            keys[span, :] = ks[k][0]
            for head in range(heads):
                flat[head, :head_width, span] = turned(vs[k][0], head, head_width)
        for head in range(heads):
            query[head, at] = jnp.where(
                lanes_of(head_width, head), qs[k][0] * scale, jnp.zeros((), dtype)
            )
    for head in range(heads):
        flat[head, head_width:, :] = jnp.ones((2 * SUB, flat.shape[2]), dtype)

    for head in range(heads):
        slope = slopes[(chunk * plane + place) * heads + head] * LOG2E
        for t in range(2 * win):
            scaled[head, t] = bias[t] * slope

    def blocks():
        for head in range(heads):
            for i in range(plane):
                first = max(0, i + plane - win)
                count = 2 * plane - first
                span = pl.ds(first * rows, count * rows)
                block = Block(
                    query[head, i], keys.at[span], flat.at[head, :, span],
                    [scaled.at[head, b - plane - i + win] for b in range(first, 2 * plane)],
                    store.at[i % 2], rows,
                )
                block.place = head, i
                yield block

    def finish(block):
        head, i = block.place
        out_ref[0, head, i, :head_width + SUB] = block.acc[:head_width + SUB]
        out_ref[0, head, i, head_width + SUB:] = block.peak

    pipeline(blocks(), finish)


def near(place, slopes, qs, ups, owns, bias, chunk0, chunks, head_width):
    plane = len(qs)
    _, rows, _ = qs[0].shape
    win = bias.shape[0] // 2
    heads = LANES // head_width
    block = (1, rows, LANES)
    pairs = chunks * heads * rows * rows * (plane * plane + plane * (plane + 1) // 2)
    key_spec = pl.BlockSpec(block, lambda c: (c, 0, 0))
    value_spec = pl.BlockSpec(block, lambda c: (chunks + c, 0, 0))
    query_spec = pl.BlockSpec(block, lambda c: (chunk0 + c, 0, 0))
    out = (chunks, heads, plane, head_width + 2 * SUB, rows)
    dtype = qs[0].dtype
    return pl.pallas_call(
        functools.partial(near_kernel, win, plane, chunk0, head_width),
        grid=(chunks,),
        in_specs=[SMEM, SMEM] + [query_spec] * plane + [key_spec] * plane + [value_spec] * plane
        + [key_spec] * plane + [value_spec] * plane
        + [pl.BlockSpec(bias.shape, lambda c: (0, 0, 0), pipeline_mode=pl.Buffered(1))],
        out_specs=pl.BlockSpec((1,) + out[1:], lambda c: (c, 0, 0, 0, 0)),
        out_shape=jax.ShapeDtypeStruct(out, jnp.float32),
        scratch_shapes=[
            pltpu.VMEM((2, 2 * win * rows, rows), jnp.float32),
            pltpu.VMEM((2 * plane * rows, LANES), dtype),
            pltpu.VMEM((heads, head_width + 2 * SUB, 2 * plane * rows), dtype),
            pltpu.VMEM((heads, plane, rows, LANES), dtype),
            pltpu.VMEM((heads, 2 * win, rows, rows), jnp.float32),
        ],
        cost_estimate=pl.CostEstimate(
            flops=4 * pairs * LANES, bytes_accessed=chunks * (4 << 20), transcendentals=pairs
        ),
        compiler_params=PARAMS,
        name="near",
    )(place, slopes, *qs, *ups, *ups, *owns, *owns, bias)


def far_kernel(win, plane, chunk0, head_width, place_ref, slopes, *refs):
    qs, dks, dvs = (refs[n * plane:(n + 1) * plane] for n in range(3))
    bias, near_ref = refs[3 * plane:3 * plane + 2]
    outs = refs[3 * plane + 2:4 * plane + 2]
    store, keys, flat, query, held, scaled = refs[4 * plane + 2:]
    place = place_ref[0]
    heads = LANES // head_width
    chunk = pl.program_id(0) + chunk0
    dtype = keys.dtype
    rows = query.shape[2]
    scale = jnp.asarray(head_width ** -0.5, dtype)
    for k in range(plane):
        at = place ^ k
        span = pl.ds(pl.multiple_of(at * rows, rows), rows)
        keys[span, :] = dks[k][0]
        for head in range(heads):
            flat[head, :head_width, span] = turned(dvs[k][0], head, head_width)
            query[head, at] = jnp.where(
                lanes_of(head_width, head), qs[k][0] * scale, jnp.zeros((), dtype)
            )
    for head in range(heads):
        flat[head, head_width:, :] = jnp.ones((2 * SUB, flat.shape[2]), dtype)
        slope = slopes[(chunk * plane + place) * heads + head] * LOG2E
        for t in range(win):
            scaled[head, t] = bias[t] * slope
    both = {}

    def blocks():
        for i in range(plane):
            count = min(plane, win - plane + i + 1)
            span = pl.ds(0, count * rows)
            for head in range(heads):
                block = Block(
                    query[head, i], keys.at[span], flat.at[head, :, span],
                    [scaled.at[head, b + plane - i - 1] for b in range(count)],
                    store.at[(i * heads + head) % 2], rows // 2,
                )
                block.place = head, i
                block.floor = near_ref[0, head, i, head_width + SUB:]
                yield block

    def finish(block):
        head, i = block.place
        acc = block.acc[:head_width + SUB].reshape(-1, SUB, rows)
        old = near_ref[0, head, i, :head_width + SUB].reshape(-1, SUB, rows)
        acc = acc + old * jnp.exp2(block.floor - block.peak)[None]
        share = 1.0 / acc[head_width // SUB:]
        both[head] = (acc[:head_width // SUB] * share).reshape(head_width, rows)
        if head == heads - 1:
            tall = jnp.concatenate([both[h] for h in range(heads)], axis=0)
            held[i ^ place] = tall.T.astype(dtype)

    pipeline(blocks(), finish)
    for k in range(plane):
        outs[k][0] = held[k]


def far(place, slopes, qs, downs, bias, before, chunk0, chunks, head_width):
    plane = len(qs)
    _, rows, _ = qs[0].shape
    win = bias.shape[0]
    heads = LANES // head_width
    block = (1, rows, LANES)
    pairs = chunks * heads * rows * rows * (plane * (plane + 1) // 2)
    key_spec = pl.BlockSpec(block, lambda c: (c, 0, 0))
    value_spec = pl.BlockSpec(block, lambda c: (chunks + c, 0, 0))
    query_spec = pl.BlockSpec(block, lambda c: (chunk0 + c, 0, 0))
    near_spec = pl.BlockSpec((1,) + before.shape[1:], lambda c: (c, 0, 0, 0, 0))
    dtype = qs[0].dtype
    return pl.pallas_call(
        functools.partial(far_kernel, win, plane, chunk0, head_width),
        grid=(chunks,),
        in_specs=[SMEM, SMEM] + [query_spec] * plane + [key_spec] * plane + [value_spec] * plane
        + [pl.BlockSpec(bias.shape, lambda c: (0, 0, 0), pipeline_mode=pl.Buffered(1))]
        + [near_spec],
        out_specs=[key_spec] * plane,
        out_shape=[jax.ShapeDtypeStruct((chunks, rows, LANES), dtype)] * plane,
        scratch_shapes=[
            pltpu.VMEM((2, plane * rows, rows), jnp.float32),
            pltpu.VMEM((plane * rows, LANES), dtype),
            pltpu.VMEM((heads, head_width + 2 * SUB, plane * rows), dtype),
            pltpu.VMEM((heads, plane, rows, LANES), dtype),
            pltpu.VMEM((plane, rows, LANES), dtype),
            pltpu.VMEM((heads, win, rows, rows), jnp.float32),
        ],
        cost_estimate=pl.CostEstimate(
            flops=4 * pairs * LANES, bytes_accessed=chunks * (4 << 20), transcendentals=pairs
        ),
        compiler_params=PARAMS,
        name="far",
    )(place, slopes, *qs, *downs, *downs, bias, before)


def per_device(queries, key_rows, values, bias_tiles, buckets, slopes):
    count = lax.axis_size("seq")
    plane = buckets.shape[0] - 1
    width = queries.shape[1]
    head_width = width // slopes.shape[0]
    chunks = width // (plane * LANES)

    def send(arrays):
        out = list(arrays[:1])
        for k, x in enumerate(arrays[1:], 1):
            pairs = [(i, i ^ k) for i in range(count)]
            out.append(lax.ppermute(x, "seq", pairs))
        return out

    def shift(arrays, step):
        pairs = [(i, (i + step * plane) % count) for i in range(count)]
        return [lax.ppermute(x, "seq", pairs) for x in arrays]

    place = (lax.axis_index("seq") % plane).astype(jnp.int32).reshape(1)

    def kv(start, size):
        span = range(start, start + size)
        return [("k", c) for c in span] + [("v", c) for c in span]

    groups = [(0, chunks - 1), (chunks - 1, 1)]
    first, second = pack(dict(k=key_rows, v=values), [kv(*g) for g in groups], plane, place)
    (query,) = pack(dict(q=queries), [[("q", c) for c in range(chunks)]], plane, place)
    owns = [send(x) for x in (first, second)]
    qs = send(query)
    near_bias, far_bias = bias_window(bias_tiles, buckets)
    ups = [shift(x, 1) for x in owns]
    downs = [shift(x, -1) for x in owns]
    sums, back = [], []
    for g, (start, size) in enumerate(groups):
        sums.append(near(place, slopes, qs, ups[g], owns[g], near_bias, start, size, head_width))
    for g, (start, size) in enumerate(groups):
        outs = far(place, slopes, qs, downs[g], far_bias, sums[g], start, size, head_width)
        back.append(send(outs))
    return unpack(place, back, 0, chunks, None)


def solution(mesh):
    rows = P(("batch", "seq"), None)
    return jax.shard_map(
        per_device,
        mesh=mesh,
        in_specs=(rows, rows, rows, P(), P(), P()),
        out_specs=rows,
        check_vma=False,
    )
```
